256 devices in a mesh: dp: 32 (over y, z_lo, core), seq: 8 (over z_hi, x).
Axes of the slice: x: 4, y: 4, z: 8 (z_hi: 2, z_lo: 4; z = z_hi * 4 + z_lo), core: 2. Of those that a mesh axis runs over, the one named last changes fastest.
Arguments:
- query: bfloat16 [36864, 2048], P(('dp', 'seq')), may hold values from -32 to 32
- key_in: bfloat16 [36864, 2048], P(('dp', 'seq')), may hold values from -6.5 to 6.5
- value: bfloat16 [36864, 2048], P(('dp', 'seq')), may hold values from -6 to 6
- out_weight: bfloat16 [2048, 3072], P('dp'), may hold values from -0.125 to 0.125
- out_grad: bfloat16 [36864, 3072], P(('dp', 'seq')), may hold values from -6 to 6
- windows: int32 [96, 5], P('dp'), may hold values from 0 to 95, as said below
- window_count: int32 [96], P('dp'), may hold values from 1 to 5, as said below
Outputs:
- output: bfloat16 [36864, 3072], P(('dp', 'seq'))
- d_query: bfloat16 [36864, 2048], P(('dp', 'seq'))
- d_key: bfloat16 [36864, 2048], P(('dp', 'seq'))
- d_value: bfloat16 [36864, 2048], P(('dp', 'seq'))
The draws below stay inside these ranges and needn't reach their ends.
Inputs may be any that keep to these rules, and one draw needn't show every extreme that they name: `windows`: row t names 5 different tiles; its first entry is t itself, and every entry lies in tile t's slab or in the slab just before or after it, a slab being 3 consecutive tiles. Tile t attends to the first window_count[t] tiles of its row; some tile attends to all 5 and some to one.
All inputs are finite; a program needn't handle non-finite values.
Results may differ from the reference program's by a relative error of at most 0.0075.
Values may be sent and summed in bfloat16 or wider, within the bound.
A program may use at most 192 MiB of HBM per device.

```python
import jax
import jax.numpy as jnp
from jax import lax

D = 3072
HD = 128
HEADS = 16
TILE = 384
WIN = 5
TPG = 3
NT = 96
TOKENS = 36864


def paired_fields(key):
    base = jax.random.fold_in(key, 11)
    streams = jax.random.split(base, 2)
    shape = (TOKENS, HEADS * HD)
    queried = 1.6 * jnp.clip(jax.random.normal(streams[0], shape, jnp.float32), -4.0, 4.0)
    keyed = 1.6 * jnp.clip(jax.random.normal(streams[1], shape, jnp.float32), -4.0, 4.0)
    return (queried, keyed)


def draw_query(key, part):
    return paired_fields(key)[0].astype(jnp.bfloat16)


def draw_key_in(key, part):
    return paired_fields(key)[1].astype(jnp.bfloat16)


def draw_windows(key, part):
    base = jax.random.fold_in(key, 23)
    tiles = jnp.arange(NT, dtype=jnp.int32)
    slab = tiles // TPG
    offsets = jnp.arange(3 * TPG, dtype=jnp.int32)
    candidate = (slab[:, None] - 1) * TPG + offsets[None, :]
    candidate_slab = slab[:, None] - 1 + offsets[None, :] // TPG
    usable = (candidate_slab >= 0) & (candidate_slab < NT // TPG) & (candidate != tiles[:, None])
    ranking = jax.random.randint(base, (NT, 3 * TPG), 0, 1 << 20, dtype=jnp.int32) * (3 * TPG) + offsets[None, :]
    boost = 1 << 29
    lower_side = usable & (offsets[None, :] // TPG == 0)
    first_score = jnp.where(lower_side, ranking + boost, jnp.where(usable, ranking, -1))
    first_pick = lax.top_k(first_score, 1)[1]
    usable_two = usable & (offsets[None, :] != first_pick)
    upper_side = usable_two & (offsets[None, :] // TPG == 2)
    second_score = jnp.where(upper_side, ranking + boost, jnp.where(usable_two, ranking, -1))
    second_pick = lax.top_k(second_score, 1)[1]
    usable_three = usable_two & (offsets[None, :] != second_pick)
    picks = [first_pick, second_pick]
    if WIN > 3:
        picks.append(lax.top_k(jnp.where(usable_three, ranking, -1), WIN - 3)[1])
    picked = jnp.concatenate(picks, axis=1)
    others = jnp.take_along_axis(candidate, picked, axis=1)
    return jnp.concatenate([tiles[:, None], others], axis=1).astype(jnp.int32)


def draw_window_count(key, part):
    filled = jax.random.randint(jax.random.fold_in(key, 31), (NT,), 3, WIN + 1, dtype=jnp.int32)
    order = jax.random.permutation(jax.random.fold_in(key, 37), NT - TPG) + TPG
    filled = filled.at[order[0]].set(WIN)
    single = jax.random.randint(jax.random.fold_in(key, 41), (), 0, TPG, dtype=jnp.int32)
    filled = filled.at[single].set(1)
    return filled.astype(jnp.int32)


def block_levels(own_key, extent, shards, least, high):
    level = 1.0
    for dim, shards_of in shards:
        steps = jax.random.uniform(jax.random.fold_in(jax.random.fold_in(own_key, 6), dim), (shards_of,), jnp.float32, least / len(shards), high / len(shards))
        level = level * jnp.repeat(jnp.exp(steps), extent[dim] // shards_of).reshape((-1,) + (1,) * (len(extent) - 1 - dim))
    return level


def normal_values(rng, shape, deviation, bound, shards=(), held_as=jnp.bfloat16):
    drawn = jax.random.normal(rng, shape, jnp.float32) * deviation
    if len(shards) > 0:
        drawn = block_levels(rng, shape, shards, -0.22, 0.18) * drawn
    return jnp.clip(drawn, min=-bound, max=bound).astype(held_as)


def setup_inputs(seed: int = 0) -> dict:
    arg_keys = jax.random.split(jax.random.key(seed), 8)
    query = draw_query(jax.random.fold_in(arg_keys[7], 71), 0)
    key_in = draw_key_in(jax.random.fold_in(arg_keys[7], 71), 0)
    value = normal_values(arg_keys[2], (TOKENS, HEADS * HD), 1.0, 6.0, ((0, 256),))
    out_weight = normal_values(arg_keys[3], (HEADS * HD, D), (HEADS * HD) ** -0.5, 0.125, ((0, 32),))
    out_grad = normal_values(arg_keys[4], (TOKENS, D), 1.0, 6.0, ((0, 256),))
    windows = draw_windows(jax.random.fold_in(arg_keys[7], 71), 0)
    window_count = draw_window_count(jax.random.fold_in(arg_keys[7], 71), 0)
    return {"query": query, "key_in": key_in, "value": value, "out_weight": out_weight, "out_grad": out_grad, "windows": windows, "window_count": window_count}


def attend_head(query, key_in, value, grad_attn, windows, window_count, head_index):
    first = (head_index * HD).astype(jnp.int32)
    query_head = lax.dynamic_slice_in_dim(query, first, HD, 1).reshape(NT, TILE, HD)
    keyed_head = lax.dynamic_slice_in_dim(key_in, first, HD, 1).reshape(NT, TILE, HD)
    value_head = lax.dynamic_slice_in_dim(value, first, HD, 1).reshape(NT, TILE, HD)
    grad_head = lax.dynamic_slice_in_dim(grad_attn, first, HD, 1).reshape(NT, TILE, HD)
    factor = HD ** -0.5

    def one_tile(tile_index):
        query_tile = query_head[tile_index]
        chosen = windows[tile_index]
        keyed_rows = keyed_head[chosen].reshape(WIN * TILE, HD)
        value_rows = value_head[chosen].reshape(WIN * TILE, HD)
        allowed = jnp.repeat(jnp.arange(WIN, dtype=jnp.int32) < window_count[tile_index], TILE)
        scores = jnp.dot(query_tile, keyed_rows.T, preferred_element_type=jnp.float32) * factor
        scores = jnp.where(allowed[None, :], scores, -jnp.inf)
        largest = jnp.max(scores, axis=1, keepdims=True)
        raised = jnp.exp(scores - largest)
        weights = raised / jnp.sum(raised, axis=1, keepdims=True)
        rounded = weights.astype(jnp.bfloat16)
        attn_tile = jnp.dot(rounded, value_rows, preferred_element_type=jnp.float32).astype(jnp.bfloat16)
        grad_tile = grad_head[tile_index]
        grad_weights = jnp.dot(grad_tile, value_rows.T, preferred_element_type=jnp.float32)
        centre = jnp.sum(weights * grad_weights, axis=1, keepdims=True)
        grad_scores = (weights * (grad_weights - centre) * factor).astype(jnp.bfloat16)
        grad_query = jnp.dot(grad_scores, keyed_rows, preferred_element_type=jnp.float32).astype(jnp.bfloat16)
        grad_keyed = jnp.dot(grad_scores.T, query_tile, preferred_element_type=jnp.float32)
        grad_valued = jnp.dot(rounded.T, grad_tile, preferred_element_type=jnp.float32)
        return attn_tile, grad_query, grad_keyed, grad_valued

    attn_tiles, query_grads, keyed_parts, valued_parts = lax.map(one_tile, jnp.arange(NT, dtype=jnp.int32))
    segments = windows.reshape(-1)
    keyed_sum = jax.ops.segment_sum(keyed_parts.reshape(NT * WIN, TILE * HD), segments, num_segments=NT)
    valued_sum = jax.ops.segment_sum(valued_parts.reshape(NT * WIN, TILE * HD), segments, num_segments=NT)
    return (attn_tiles.reshape(TOKENS, HD), query_grads.reshape(TOKENS, HD),
            keyed_sum.reshape(TOKENS, HD).astype(jnp.bfloat16), valued_sum.reshape(TOKENS, HD).astype(jnp.bfloat16))


def merge_heads(stacked):
    return jnp.transpose(stacked, (1, 0, 2)).reshape(TOKENS, HEADS * HD)


def reference(query, key_in, value, out_weight, out_grad, windows, window_count):
    grad_attn = jnp.dot(out_grad, out_weight.T, preferred_element_type=jnp.float32).astype(jnp.bfloat16)

    def per_head(head_index):
        return attend_head(query, key_in, value, grad_attn, windows, window_count, head_index)

    attn_all, query_all, keyed_all, valued_all = lax.map(per_head, jnp.arange(HEADS, dtype=jnp.int32))
    attn = merge_heads(attn_all)
    output = jnp.dot(attn, out_weight, preferred_element_type=jnp.float32).astype(jnp.bfloat16)
    return output, merge_heads(query_all), merge_heads(keyed_all), merge_heads(valued_all)
```

```python
import jax, jax.numpy as jnp
from jax import lax
from jax.experimental import pallas as pl
from jax.experimental.pallas import tpu as pltpu
from jax.sharding import PartitionSpec as P
HD=128; TILE=384; WIN=5
LOG2E=1.4426950408889634
def dotT(a,b): return lax.dot_general(a,b,(((1,),(1,)),((),())),preferred_element_type=jnp.float32)
def dot0(a,b): return lax.dot_general(a,b,(((0,),(0,)),((),())),preferred_element_type=jnp.float32)
def dot(a,b): return jnp.dot(a,b,preferred_element_type=jnp.float32)

def attend(ids, counts, q_ref, g_ref, k_ref, v_ref, attn_ref, dq_ref, dk_ref, dv_ref, s_buf, e_buf):
    factor = HD ** -0.5
    t = pl.program_id(1)
    @pl.when(t == 0)
    def _():
        dk_ref[...] = jnp.zeros_like(dk_ref)
        dv_ref[...] = jnp.zeros_like(dv_ref)
    q = q_ref[...]; g = g_ref[...]
    count = counts[t]
    top = None
    for j in range(WIN):
        rows = pl.ds(pl.multiple_of(ids[t, j] * TILE, TILE), TILE)
        s = dotT(q, k_ref[rows, :])
        if j > 0:
            s = s + jnp.where(j < count, 0.0, -jnp.inf).astype(jnp.float32)
        s_buf[j] = s
        m = jnp.max(s, axis=1, keepdims=True)
        top = m if top is None else jnp.maximum(top, m)
    total = jnp.zeros((TILE, 1), jnp.float32)
    acc = jnp.zeros((TILE, HD), jnp.float32)
    for j in range(WIN):
        rows = pl.ds(pl.multiple_of(ids[t, j] * TILE, TILE), TILE)
        e = jnp.exp2((s_buf[j] - top) * (factor * LOG2E))
        total = total + jnp.sum(e, axis=1, keepdims=True)
        eb = e.astype(jnp.bfloat16)
        e_buf[j] = eb
        acc = acc + dot(eb, v_ref[rows, :])
    inv = 1.0 / total
    attn = acc * inv
    attn_ref[...] = attn.astype(jnp.bfloat16)
    gf = g.astype(jnp.float32)
    centre = jnp.sum(gf * attn, axis=1, keepdims=True)
    gs = (gf * inv).astype(jnp.bfloat16)
    qs = (q.astype(jnp.float32) * (inv * factor)).astype(jnp.bfloat16)
    dq = jnp.zeros((TILE, HD), jnp.float32)
    for j in range(WIN):
        rows = pl.ds(pl.multiple_of(ids[t, j] * TILE, TILE), TILE)
        dp = dotT(g, v_ref[rows, :])
        eb = e_buf[j]
        ds = (eb.astype(jnp.float32) * (dp - centre)).astype(jnp.bfloat16)
        dq = dq + dot(ds, k_ref[rows, :])
        dk_ref[rows, :] += dot0(ds, qs)
        dv_ref[rows, :] += dot0(eb, gs)
    dq_ref[...] = (dq * (inv * factor)).astype(jnp.bfloat16)

def attention(q, g, k, v, ids, counts):
    rows, width = q.shape
    ext = k.shape[0]
    heads = width // HD; tiles = rows // TILE
    qs = pl.BlockSpec((TILE, HD), lambda h, t, *_: (t, h))
    ks = pl.BlockSpec((ext, HD), lambda h, t, *_: (0, h))
    bf = jax.ShapeDtypeStruct((rows, width), jnp.bfloat16)
    f32 = jax.ShapeDtypeStruct((ext, width), jnp.float32)
    return pl.pallas_call(
        attend,
        grid_spec=pltpu.PrefetchScalarGridSpec(
            num_scalar_prefetch=2, grid=(heads, tiles),
            in_specs=[qs, qs, ks, ks], out_specs=[qs, qs, ks, ks],
            scratch_shapes=[pltpu.VMEM((WIN, TILE, TILE), jnp.float32), pltpu.VMEM((WIN, TILE, TILE), jnp.bfloat16)]),
        out_shape=[bf, bf, f32, f32],
        compiler_params=pltpu.CompilerParams(vmem_limit_bytes=60 << 20),
        cost_estimate=pl.CostEstimate(flops=7_000_000_000*6, bytes_accessed=14_000_000, transcendentals=4_400_000),
    )(ids, counts, q, g, k, v)


def to_heads(x):
    return lax.all_to_all(x, "seq", split_axis=1, concat_axis=0, tiled=True)


def to_tokens(x):
    return lax.all_to_all(x, "seq", split_axis=0, concat_axis=1, tiled=True)


def with_neighbours(block, low_part, high_part):
    count = lax.axis_size("dp")
    up = [(i, i + 1) for i in range(count - 1)]
    down = [(b, a) for a, b in up]
    return lax.ppermute(low_part, "dp", up), lax.ppermute(high_part, "dp", down)


def body(query, key_in, value, out_weight, out_grad, windows, window_count):
    tiles = windows.shape[0]
    weight = lax.all_gather(out_weight, "dp", axis=0, tiled=True)
    k = to_heads(key_in)
    v = to_heads(value)
    kv = jnp.concatenate([k, v], axis=1)
    low, high = with_neighbours(kv, kv, kv)
    ext = jnp.concatenate([low, kv, high], axis=0)
    width = k.shape[1]
    rows = k.shape[0]
    q = to_heads(query)
    grad_tokens = lax.dot_general(out_grad, weight, (((1,), (1,)), ((), ())),
                                  preferred_element_type=jnp.float32).astype(jnp.bfloat16)
    g = to_heads(grad_tokens)
    ids = windows - (lax.axis_index("dp") - 1) * tiles
    attn, dq, dk, dv = attention(q, g, ext[:, :width], ext[:, width:], ids, window_count)
    attn_tokens = to_tokens(attn)
    d_kv = jnp.concatenate([dk, dv], axis=1)
    rim = d_kv.astype(jnp.bfloat16)
    low, high = with_neighbours(None, rim[2 * rows:], rim[:rows])
    output = jnp.dot(attn_tokens, weight, preferred_element_type=jnp.float32).astype(jnp.bfloat16)
    d_query = to_tokens(dq)
    summed = (d_kv[rows:2 * rows] + low.astype(jnp.float32) + high.astype(jnp.float32)).astype(jnp.bfloat16)
    return output, d_query, to_tokens(summed[:, :width]), to_tokens(summed[:, width:])


def solution(mesh):
    both = P(("dp", "seq"), None)
    return jax.shard_map(
        body, mesh=mesh, check_vma=False,
        in_specs=(both, both, both, P("dp", None), both, P("dp", None), P("dp")),
        out_specs=(both, both, both, both),
    )
```

```python
import jax
import jax.numpy as jnp
from jax import lax
from jax.experimental import pallas as pl
from jax.experimental.pallas import tpu as pltpu
from jax.sharding import PartitionSpec as P

HD = 128
TILE = 384
WIN = 5
LOG2E = 1.4426950408889634
MESH = pl.DeviceIdType.MESH
BF16 = jnp.bfloat16
F32 = jnp.float32


def dotT(a, b):
    return lax.dot_general(a, b, (((1,), (1,)), ((), ())), preferred_element_type=F32)


def dot0(a, b):
    return lax.dot_general(a, b, (((0,), (0,)), ((), ())), preferred_element_type=F32)


def dot(a, b):
    return jnp.dot(a, b, preferred_element_type=F32)


def flip(dp, index):
    return lax.rem(index + 4 * lax.rem(dp // 8, 2), 8)


def ring(index, step, count):
    return lax.rem(index + step + count, count)


def rows_of(index, count):
    return pl.ds(pl.multiple_of(index * count, count), count)


def pair_columns(pair):
    return pl.ds(pl.multiple_of(pair * 256, 256), 256)


def remote(src, dst, send, recv, device):
    return pltpu.make_async_remote_copy(
        src_ref=src, dst_ref=dst, send_sem=send, recv_sem=recv, device_id=device, device_id_type=MESH
    )


def greet(partners):
    barrier = pltpu.get_barrier_semaphore()
    for device in partners:
        pl.semaphore_signal(barrier, inc=1, device_id=device, device_id_type=MESH)
    pl.semaphore_wait(barrier, len(partners))


SIDES = ((-1, 2), (1, 0))


def collect(q_ref, k_ref, v_ref, w_ref, og_ref, q_out, k_out, v_out, g_out, w_out,
            g_stage, w_buf, a_send, a_recv, h_send, h_recv, g_send, g_recv,
            wz_send, wz_recv, wx_send, wx_recv, wy_send, wy_recv, wq_send, wq_recv,
            wxx_send, wxx_recv, sib_send, sib_recv, own_sem, load_sem):
    dp = lax.axis_index("dp")
    seq = lax.axis_index("seq")
    y, z_lo, core = dp // 8, lax.rem(dp // 2, 4), lax.rem(dp, 2)
    x = lax.rem(seq, 4)
    z = (seq // 4) * 4 + z_lo
    pair = flip(dp, seq)
    tokens = q_ref.shape[0]
    share = w_ref.shape[0]
    quarter = share // 4

    def along_z(step):
        to = lax.rem(z + step + 8, 8)
        return (y * 8 + lax.rem(to, 4) * 2 + core, (to // 4) * 4 + x)

    def along_y(step):
        return (lax.rem(y + step + 4, 4) * 8 + lax.rem(dp, 8), seq)

    def along_x(step):
        return (dp, (seq // 4) * 4 + lax.rem(x + step + 4, 4))

    sibling = (dp + 1 - 2 * core, seq)
    far = 2 - 4 * core
    beside = [(ring(dp, step, 32), flip(ring(dp, step, 32), pair)) for step, _ in SIDES]
    greet([(dp, ring(seq, r, 8)) for r in range(1, 8)] + beside
          + [along_z(1), along_z(-1), along_z(2), along_z(-2)]
          + [along_y(1), along_y(-1), along_y(2), sibling])

    z_off = (0, -1, 1, 2)
    y_off = (0, -1, 1, 2)

    def shard(o, i, mine=True):
        c = core if mine else 1 - core
        return lax.rem(y + y_off[o] + 4, 4) * 8 + lax.rem(z_lo + z_off[i] + 4, 4) * 2 + c

    def whole(o, i, mine=True):
        return w_out.at[rows_of(shard(o, i, mine), share), :]

    def part(o, i, of_x):
        return w_out.at[rows_of(shard(o, i) * 4 + of_x, quarter), :]

    def x_from(j):
        return lax.rem(x - j + 4, 4)

    own_quarter = w_ref.at[rows_of(x, quarter), :]
    pending = []

    def go(copy):
        copy.start()
        pending.append(copy)

    def send_z(i, step):
        return remote(own_quarter, part(0, 0, x), wz_send.at[i], wz_recv.at[i], along_z(step))

    def got_z(i):
        return remote(own_quarter, part(0, i + 1, x), wz_send.at[i], wz_recv.at[i], along_z(1))

    go(send_z(0, 1))
    go(send_z(1, -1))
    go(send_z(2, far))

    def send_y(i, src):
        go(remote(src, whole(0, i), wy_send.at[0, i], wy_recv.at[0, i], along_y(1)))
        go(remote(src, whole(0, i), wy_send.at[1, i], wy_recv.at[1, i], along_y(-1)))

    def send_sibling(o, i, src):
        go(remote(src, whole(o, i), sib_send.at[o * 4 + i], sib_recv.at[o * 4 + i], sibling))

    def send_across(i, src):
        go(remote(src, part(0, i, x), wq_send.at[i], wq_recv.at[i], along_y(2)))

    send_across(0, own_quarter)
    send_y(0, w_ref)
    send_sibling(0, 0, w_ref)
    keep = pltpu.make_async_copy(w_ref, whole(0, 0), own_sem.at[3])
    keep.start()

    ext = 8 * tokens

    def landing(out, index, place):
        if place is None:
            return out.at[rows_of(index, tokens), :]
        return out.at[pl.ds(pl.multiple_of(place * ext + index * tokens, tokens), tokens), :]

    sources = ((k_ref, k_out, 1), (v_ref, v_out, 1), (q_ref, q_out, None))

    def exchange(n, r):
        ref, out, place = sources[n]
        to = ring(seq, r, 8)
        block = ref.at[:, pair_columns(flip(dp, to))]
        return remote(block, landing(out, seq, place), a_send.at[n, r], a_recv.at[n, r], (dp, to))

    def arrival(n, r):
        ref, out, place = sources[n]
        src = ring(seq, -r, 8)
        return remote(ref.at[:, pair_columns(pair)], landing(out, src, place), a_send.at[n, r],
                      a_recv.at[n, r], (dp, src))

    def pass_on(n, r, src):
        _, out, _ = sources[n]
        index = ring(seq, -r, 8)
        for side in range(2):
            go(remote(src, landing(out, index, SIDES[side][1]), h_send.at[side, n, r],
                      h_recv.at[side, n, r], beside[side]))

    def passed(n, r, side):
        out = sources[n][1]
        index = ring(flip(beside[side][0], pair), -r, 8)
        return remote(out.at[pl.ds(0, tokens), :], landing(out, index, SIDES[1 - side][1]),
                      h_send.at[1 - side, n, r], h_recv.at[1 - side, n, r], beside[side])

    far_first = (4, 3, 5, 2, 6, 1, 7)
    keeps = [keep]
    for n in range(3):
        ref, out, place = sources[n]
        mine = pltpu.make_async_copy(ref.at[:, pair_columns(pair)], landing(out, seq, place), own_sem.at[n])
        mine.start()
        keeps.append(mine)
    for n in range(2):
        for r in far_first:
            go(exchange(n, r))
    for n in range(2):
        pass_on(n, 0, sources[n][0].at[:, pair_columns(pair)])
    for r in far_first:
        go(exchange(2, r))

    for i in range(3):
        got_z(i).wait_recv()
        piece = part(0, i + 1, x)
        for j in range(1, 4):
            go(remote(piece, piece, wx_send.at[i, j - 1], wx_recv.at[i, j - 1], along_x(j)))
        send_across(i + 1, piece)
    for r in (1, 7):
        for n in range(2):
            arrival(n, r).wait_recv()
            pass_on(n, r, landing(sources[n][1], ring(seq, -r, 8), 1))
    for i in range(3):
        for j in range(1, 4):
            piece = part(0, i + 1, x_from(j))
            remote(piece, piece, wx_send.at[i, j - 1], wx_recv.at[i, j - 1], along_x(-j)).wait_recv()
        send_y(i + 1, whole(0, i + 1))
        send_sibling(0, i + 1, whole(0, i + 1))
    for r in (4, 3, 5, 2, 6):
        for n in range(2):
            arrival(n, r).wait_recv()
            pass_on(n, r, landing(sources[n][1], ring(seq, -r, 8), 1))
    for i in range(4):
        piece = part(3, i, x)
        remote(piece, piece, wq_send.at[i], wq_recv.at[i], along_y(2)).wait_recv()
        for j in range(1, 4):
            go(remote(piece, piece, wxx_send.at[i, j - 1], wxx_recv.at[i, j - 1], along_x(j)))
        for o in (1, 2):
            block = whole(o, i)
            remote(block, block, wy_send.at[o - 1, i], wy_recv.at[o - 1, i], along_y(y_off[o])).wait_recv()
            send_sibling(o, i, block)

    grads = []

    def project(o):
        for i in range(4):
            block = whole(o, i, False)
            remote(block, block, sib_send.at[o * 4 + i], sib_recv.at[o * 4 + i], sibling).wait_recv()
        base = 2 * lax.rem(y + y_off[o] + 4, 4)
        loads = [pltpu.make_async_copy(w_out.at[rows_of(base + b, 256), :], w_buf.at[b], load_sem.at[b])
                 for b in range(2)]
        for load in loads:
            load.start()
        for b in range(2):
            loads[b].wait()
            g_stage[2 * o + b] = dotT(og_ref[...], w_buf[b]).astype(BF16)
        for b in range(2):
            to = flip(dp, base + b)

            @pl.when(to != seq)
            def _():
                remote(g_stage.at[2 * o + b], g_out.at[rows_of(seq, tokens), :], g_send.at[2 * o + b],
                       g_recv.at[seq], (dp, to)).start()

            @pl.when(to == seq)
            def _():
                pltpu.make_async_copy(g_stage.at[2 * o + b], g_out.at[rows_of(seq, tokens), :], g_send.at[2 * o + b]).start()

            grads.append((2 * o + b, to))

    keep.wait()
    keeps.pop(0)
    project(0)
    for i in range(4):
        for j in range(1, 4):
            piece = part(3, i, x_from(j))
            remote(piece, piece, wxx_send.at[i, j - 1], wxx_recv.at[i, j - 1], along_x(-j)).wait_recv()
        send_sibling(3, i, whole(3, i))
    project(1)
    project(2)
    project(3)

    for copy in keeps:
        copy.wait()
    for r in far_first:
        arrival(2, r).wait_recv()
    for n in range(2):
        for r in range(8):
            for side in range(2):
                passed(n, r, side).wait_recv()
    for r in range(1, 8):
        src = ring(seq, -r, 8)
        remote(g_stage.at[0], g_out.at[rows_of(src, tokens), :], g_send.at[0], g_recv.at[src], (dp, src)).wait_recv()
    for slot, to in grads:

        @pl.when(to != seq)
        def _():
            remote(g_stage.at[slot], g_out.at[rows_of(seq, tokens), :], g_send.at[slot], g_recv.at[seq],
                   (dp, to)).wait_send()

        @pl.when(to == seq)
        def _():
            pltpu.make_async_copy(g_stage.at[slot], g_out.at[rows_of(seq, tokens), :], g_send.at[slot]).wait()
    for copy in pending:
        copy.wait_send()


def gather(query, key_in, value, out_weight, out_grad):
    tokens, width = query.shape
    rows = 8 * tokens
    vm = pl.BlockSpec(memory_space=pltpu.VMEM)
    hbm = pl.BlockSpec(memory_space=pl.ANY)
    sem = pltpu.SemaphoreType.DMA
    slab = jax.ShapeDtypeStruct((rows, 256), BF16)
    three = jax.ShapeDtypeStruct((3 * rows, 256), BF16)
    pairs = [(3, 8), (2, 2, 8), (8,), (3,), (3, 3), (2, 4), (4,), (4, 3), (16,)]
    return pl.pallas_call(
        collect,
        out_shape=[slab, three, three, slab, jax.ShapeDtypeStruct((32 * out_weight.shape[0], out_weight.shape[1]), BF16)],
        in_specs=[vm] * 5,
        out_specs=[hbm] * 5,
        scratch_shapes=[pltpu.VMEM((8, tokens, 256), BF16), pltpu.VMEM((2, 256, out_weight.shape[1]), BF16)]
        + [sem(p) for p in pairs for _ in range(2)] + [sem((4,)), sem((2,))],
        compiler_params=pltpu.CompilerParams(collective_id=0, has_side_effects=True, vmem_limit_bytes=40 << 20),
    )(query, key_in, value, out_weight, out_grad)


def deliver(attn_ref, dq_ref, dk_ref, dv_ref, rk_ref, rv_ref, w_ref, o_out, q_out, k_out, v_out,
            tok, own, low, high, stage, w_buf, a_send, a_recv, q_send, q_recv, h_send, h_recv,
            s_send, s_recv, own_sem, w_sem, f_sem):
    dp = lax.axis_index("dp")
    seq = lax.axis_index("seq")
    pair = flip(dp, seq)
    tokens = o_out.shape[0]
    beside = [(ring(dp, step, 32), flip(ring(dp, step, 32), pair)) for step, _ in SIDES]
    loads = [pltpu.make_async_copy((dk_ref, dv_ref)[n], own.at[n], f_sem.at[n]) for n in range(2)]
    for load in loads:
        load.start()
    cut = w_buf.shape[2]
    chunks = [pltpu.make_async_copy(w_ref.at[:, pl.ds(c * cut, cut)], w_buf.at[c], w_sem.at[c])
              for c in range(w_buf.shape[0])]
    greet([(dp, ring(seq, r, 8)) for r in range(1, 8)] + beside)
    pending = []

    def go(copy):
        copy.start()
        pending.append(copy)

    rims = (rk_ref, rv_ref)
    far_first = (4, 3, 5, 2, 6, 1, 7, 0)
    into = (high, low)

    def rim(n, r, side):
        index = ring(seq, r, 8)
        return remote(rims[n].at[side, rows_of(index, tokens), :], into[side].at[n, rows_of(index, tokens), :],
                      h_send.at[side, n, index], h_recv.at[side, n, index], beside[side])

    for r in far_first:
        for n in range(2):
            for side in range(2):
                go(rim(n, r, side))

    def tokens_at(index):
        return rows_of(index, tokens)

    for r in far_first[:-1]:
        to = ring(seq, r, 8)
        go(remote(attn_ref.at[tokens_at(to), :], tok.at[:, pair_columns(pair)], a_send.at[r], a_recv.at[r], (dp, to)))
    for r in far_first[:-1]:
        to = ring(seq, r, 8)
        go(remote(dq_ref.at[tokens_at(to), :], q_out.at[:, pair_columns(pair)], q_send.at[r], q_recv.at[r], (dp, to)))
    keeps = [pltpu.make_async_copy(attn_ref.at[tokens_at(seq), :], tok.at[:, pair_columns(pair)], own_sem.at[0]),
             pltpu.make_async_copy(dq_ref.at[tokens_at(seq), :], q_out.at[:, pair_columns(pair)], own_sem.at[1])]
    for copy in keeps:
        copy.start()
    for chunk in chunks:
        chunk.start()
    for load in loads:
        load.wait()
    outs = (k_out, v_out)

    def send_sum(r):
        to = ring(seq, r, 8)
        for n in range(2):
            if r:
                go(remote(stage.at[n, tokens_at(to), :], outs[n].at[:, pair_columns(pair)], s_send.at[n, r],
                          s_recv.at[n, r], (dp, to)))
            else:
                copy = pltpu.make_async_copy(stage.at[n, tokens_at(to), :], outs[n].at[:, pair_columns(pair)], own_sem.at[2 + n])
                copy.start()
                keeps.append(copy)

    last = None
    for r in far_first:
        index = ring(seq, r, 8)
        at = tokens_at(index)
        for n in range(2):
            for side in range(2):
                remote(rims[n].at[side, at, :], into[side].at[n, at, :], h_send.at[side, n, index],
                       h_recv.at[side, n, index], beside[1 - side]).wait_recv()
            stage[n, at, :] = (own[n, at, :] + low[n, at, :].astype(F32) + high[n, at, :].astype(F32)).astype(BF16)
        if last is not None:
            send_sum(last)
        last = r
    send_sum(last)

    keeps[0].wait()
    keeps.pop(0)
    for r in far_first[:-1]:
        src = ring(seq, -r, 8)
        remote(attn_ref.at[tokens_at(src), :], tok.at[:, pair_columns(flip(dp, src))], a_send.at[r], a_recv.at[r], (dp, src)).wait_recv()
    for c in range(len(chunks)):
        chunks[c].wait()
        o_out[:, c * cut:(c + 1) * cut] = dot(tok[...], w_buf[c]).astype(BF16)
    for copy in keeps:
        copy.wait()
    for r in far_first[:-1]:
        src = ring(seq, -r, 8)
        columns = pair_columns(flip(dp, src))
        remote(dq_ref.at[tokens_at(src), :], q_out.at[:, columns], q_send.at[r], q_recv.at[r], (dp, src)).wait_recv()
        for n in range(2):
            remote(stage.at[n, tokens_at(src), :], outs[n].at[:, columns], s_send.at[n, r], s_recv.at[n, r], (dp, src)).wait_recv()
    for copy in pending:
        copy.wait_send()


def scatter(attn, dq, dk, dv, rk, rv, weight):
    rows, width = attn.shape
    tokens = rows // 8
    depth = weight.shape[1]
    vm = pl.BlockSpec(memory_space=pltpu.VMEM)
    hbm = pl.BlockSpec(memory_space=pl.ANY)
    sem = pltpu.SemaphoreType.DMA
    wide = jax.ShapeDtypeStruct((tokens, 8 * width), BF16)
    cut = 512
    pairs = [(8,), (8,), (2, 2, 8), (2, 8)]
    return pl.pallas_call(
        deliver,
        out_shape=[jax.ShapeDtypeStruct((tokens, depth), BF16), wide, wide, wide],
        in_specs=[hbm] * 7,
        out_specs=[vm] * 4,
        scratch_shapes=[
            pltpu.VMEM((tokens, 8 * width), BF16), pltpu.VMEM((2, rows, width), F32), pltpu.VMEM((2, rows, width), BF16),
            pltpu.VMEM((2, rows, width), BF16), pltpu.VMEM((2, rows, width), BF16), pltpu.VMEM((depth // cut, weight.shape[0], cut), BF16)]
        + [sem(p) for p in pairs for _ in range(2)] + [sem((4,)), sem((depth // cut,)), sem((2,))],
        compiler_params=pltpu.CompilerParams(collective_id=1, has_side_effects=True, vmem_limit_bytes=48 << 20),
    )(attn, dq, dk, dv, rk, rv, weight)


def attend(ids, counts, q_ref, g_ref, k_ref, v_ref, attn_ref, dq_ref, dk_out, dv_out, rk_out, rv_out,
           s_buf, e_buf, dk_ref, dv_ref):
    factor = HD ** -0.5
    t = pl.program_id(1)
    @pl.when(t == 0)
    def _():
        dk_ref[...] = jnp.zeros_like(dk_ref)
        dv_ref[...] = jnp.zeros_like(dv_ref)
    q = q_ref[...]; g = g_ref[...]
    count = counts[t]
    top = None
    for j in range(WIN):
        rows = pl.ds(pl.multiple_of(ids[t, j] * TILE, TILE), TILE)
        s = dotT(q, k_ref[rows, :])
        if j > 0:
            s = s + jnp.where(j < count, 0.0, -jnp.inf).astype(jnp.float32)
        s_buf[j] = s
        m = jnp.max(s, axis=1, keepdims=True)
        top = m if top is None else jnp.maximum(top, m)
    total = jnp.zeros((TILE, 1), jnp.float32)
    acc = jnp.zeros((TILE, HD), jnp.float32)
    for j in range(WIN):
        rows = pl.ds(pl.multiple_of(ids[t, j] * TILE, TILE), TILE)
        e = jnp.exp2((s_buf[j] - top) * (factor * LOG2E))
        total = total + jnp.sum(e, axis=1, keepdims=True)
        eb = e.astype(jnp.bfloat16)
        e_buf[j] = eb
        acc = acc + dot(eb, v_ref[rows, :])
    inv = 1.0 / total
    attn = acc * inv
    attn_ref[...] = attn.astype(jnp.bfloat16)
    gf = g.astype(jnp.float32)
    centre = jnp.sum(gf * attn, axis=1, keepdims=True)
    gs = (gf * inv).astype(jnp.bfloat16)
    qs = (q.astype(jnp.float32) * (inv * factor)).astype(jnp.bfloat16)
    dq = jnp.zeros((TILE, HD), jnp.float32)
    for j in range(WIN):
        rows = pl.ds(pl.multiple_of(ids[t, j] * TILE, TILE), TILE)
        dp = dotT(g, v_ref[rows, :])
        eb = e_buf[j]
        ds = (eb.astype(jnp.float32) * (dp - centre)).astype(jnp.bfloat16)
        dq = dq + dot(ds, k_ref[rows, :])
        dk_ref[rows, :] += dot0(ds, qs)
        dv_ref[rows, :] += dot0(eb, gs)
    dq_ref[...] = (dq * (inv * factor)).astype(jnp.bfloat16)

    @pl.when(t == pl.num_programs(1) - 1)
    def _():
        n = dk_out.shape[0]
        for acc_ref, own, rim in ((dk_ref, dk_out, rk_out), (dv_ref, dv_out, rv_out)):
            rim[0] = acc_ref[:n, :].astype(jnp.bfloat16)
            own[...] = acc_ref[n:2 * n, :]
            rim[1] = acc_ref[2 * n:, :].astype(jnp.bfloat16)

def attention(q, g, k, v, ids, counts):
    rows, width = q.shape
    ext = k.shape[0]
    heads = width // HD
    tiles = rows // TILE
    qs = pl.BlockSpec((TILE, HD), lambda h, t, *_: (t, h))
    ks = pl.BlockSpec((ext, HD), lambda h, t, *_: (0, h))
    own = pl.BlockSpec((rows, HD), lambda h, t, *_: (0, h))
    rim = pl.BlockSpec((2, rows, HD), lambda h, t, *_: (0, 0, h))
    bf = jax.ShapeDtypeStruct((rows, width), jnp.bfloat16)
    f32 = jax.ShapeDtypeStruct((rows, width), jnp.float32)
    rims = jax.ShapeDtypeStruct((2, rows, width), jnp.bfloat16)
    return pl.pallas_call(
        attend,
        grid_spec=pltpu.PrefetchScalarGridSpec(
            num_scalar_prefetch=2, grid=(heads, tiles),
            in_specs=[qs, qs, ks, ks], out_specs=[qs, qs, own, own, rim, rim],
            scratch_shapes=[pltpu.VMEM((WIN, TILE, TILE), jnp.float32), pltpu.VMEM((WIN, TILE, TILE), jnp.bfloat16),
                            pltpu.VMEM((ext, HD), jnp.float32), pltpu.VMEM((ext, HD), jnp.float32)]),
        out_shape=[bf, bf, f32, f32, rims, rims],
        compiler_params=pltpu.CompilerParams(vmem_limit_bytes=60 << 20),
    )(ids, counts, q, g, k, v)


def body(query, key_in, value, out_weight, out_grad, windows, window_count):
    q, k, v, g, weight = gather(query, key_in, value, out_weight, out_grad)
    ids = windows - (lax.axis_index("dp") - 1) * windows.shape[0]
    attn, dq, dk, dv, rk, rv = attention(q, g, k, v, ids, window_count)
    return tuple(scatter(attn, dq, dk, dv, rk, rv, weight))


def solution(mesh):
    both = P(("dp", "seq"), None)
    return jax.shard_map(
        body, mesh=mesh, check_vma=False,
        in_specs=(both, both, both, P("dp", None), both, P("dp", None), P("dp")),
        out_specs=(both, both, both, both),
    )
```

```python
import jax
import jax.numpy as jnp
from jax import lax
from jax.experimental import pallas as pl
from jax.experimental.pallas import tpu as pltpu
from jax.sharding import PartitionSpec as P

HD = 128
TILE = 384
WIN = 5
LOG2E = 1.4426950408889634
MESH = pl.DeviceIdType.MESH
BF16 = jnp.bfloat16
F32 = jnp.float32


def dotT(a, b):
    return lax.dot_general(a, b, (((1,), (1,)), ((), ())), preferred_element_type=F32)


def dot0(a, b):
    return lax.dot_general(a, b, (((0,), (0,)), ((), ())), preferred_element_type=F32)


def dot(a, b):
    return jnp.dot(a, b, preferred_element_type=F32)


def flip(dp, index):
    return lax.rem(index + 4 * lax.rem(dp // 8, 2), 8)


def ring(index, step, count):
    return lax.rem(index + step + count, count)


def rows_of(index, count):
    return pl.ds(pl.multiple_of(index * count, count), count)


def pair_columns(pair):
    return pl.ds(pl.multiple_of(pair * 256, 256), 256)


def remote(src, dst, send, recv, device):
    return pltpu.make_async_remote_copy(
        src_ref=src, dst_ref=dst, send_sem=send, recv_sem=recv, device_id=device, device_id_type=MESH
    )


def greet(partners):
    barrier = pltpu.get_barrier_semaphore()
    for device in partners:
        pl.semaphore_signal(barrier, inc=1, device_id=device, device_id_type=MESH)
    pl.semaphore_wait(barrier, len(partners))


SIDES = ((-1, 2), (1, 0))


def layer(win_ref, count_ref, q_ref, k_ref, v_ref, w_ref, og_in, o_out, dq_out, dk_out, dv_out,
          q_buf, k_out, v_out, g_out, w_out, og_ref, g_stage, s_buf, e_buf, attn_f, inv_f, attn_b, dq_b,
          pieces, own, k_tile, v_tile, rim_buf, low, high, stage, tok,
          a_send, a_recv, h_send, h_recv, g_send, g_recv,
          wz_send, wz_recv, wx_send, wx_recv, wy_send, wy_recv, wq_send, wq_recv,
          wxx_send, wxx_recv, sib_send, sib_recv, t_send, t_recv, d_send, d_recv, r_send, r_recv,
          s_send, s_recv, own_sem):
    dp = lax.axis_index("dp")
    seq = lax.axis_index("seq")
    y, z_lo, core = dp // 8, lax.rem(dp // 2, 4), lax.rem(dp, 2)
    x = lax.rem(seq, 4)
    z = (seq // 4) * 4 + z_lo
    pair = flip(dp, seq)
    tokens = q_ref.shape[0]
    share = w_ref.shape[0]
    quarter = share // 4

    def along_z(step):
        to = lax.rem(z + step + 8, 8)
        return (y * 8 + lax.rem(to, 4) * 2 + core, (to // 4) * 4 + x)

    def along_y(step):
        return (lax.rem(y + step + 4, 4) * 8 + lax.rem(dp, 8), seq)

    def along_x(step):
        return (dp, (seq // 4) * 4 + lax.rem(x + step + 4, 4))

    sibling = (dp + 1 - 2 * core, seq)
    far = 2 - 4 * core
    beside = [(ring(dp, step, 32), flip(ring(dp, step, 32), pair)) for step, _ in SIDES]
    greet([(dp, ring(seq, r, 8)) for r in range(1, 8)] + beside
          + [along_z(1), along_z(-1), along_z(2), along_z(-2)]
          + [along_y(1), along_y(-1), along_y(2), sibling])

    z_off = (0, -1, 1, 2)
    y_off = (0, -1, 1, 2)

    def shard(o, i, mine=True):
        c = core if mine else 1 - core
        return lax.rem(y + y_off[o] + 4, 4) * 8 + lax.rem(z_lo + z_off[i] + 4, 4) * 2 + c

    def whole(o, i, mine=True):
        return w_out.at[rows_of(shard(o, i, mine), share), :]

    def part(o, i, of_x):
        return w_out.at[rows_of(shard(o, i) * 4 + of_x, quarter), :]

    def x_from(j):
        return lax.rem(x - j + 4, 4)

    og_load = pltpu.make_async_copy(og_in, og_ref, own_sem.at[4])
    og_load.start()
    own_quarter = w_ref.at[rows_of(x, quarter), :]
    pending = []

    def go(copy):
        copy.start()
        pending.append(copy)

    def send_z(i, step):
        return remote(own_quarter, part(0, 0, x), wz_send.at[i], wz_recv.at[i], along_z(step))

    def got_z(i):
        return remote(own_quarter, part(0, i + 1, x), wz_send.at[i], wz_recv.at[i], along_z(1))

    go(send_z(0, 1))
    go(send_z(1, -1))
    go(send_z(2, far))

    def send_y(i, src):
        go(remote(src, whole(0, i), wy_send.at[0, i], wy_recv.at[0, i], along_y(1)))
        go(remote(src, whole(0, i), wy_send.at[1, i], wy_recv.at[1, i], along_y(-1)))

    def send_sibling(o, i, src):
        go(remote(src, whole(o, i), sib_send.at[o * 4 + i], sib_recv.at[o * 4 + i], sibling))

    def send_across(i, src):
        go(remote(src, part(0, i, x), wq_send.at[i], wq_recv.at[i], along_y(2)))

    send_across(0, own_quarter)
    send_y(0, w_ref)
    send_sibling(0, 0, w_ref)
    keep = pltpu.make_async_copy(w_ref, whole(0, 0), own_sem.at[3])
    keep.start()

    ext = 8 * tokens

    def landing(out, index, place):
        if place is None:
            return out.at[rows_of(index, tokens), :]
        return out.at[pl.ds(pl.multiple_of(place * ext + index * tokens, tokens), tokens), :]

    sources = ((k_ref, k_out, 1), (v_ref, v_out, 1), (q_ref, q_buf, None))

    def exchange(n, r):
        ref, out, place = sources[n]
        to = ring(seq, r, 8)
        block = ref.at[:, pair_columns(flip(dp, to))]
        return remote(block, landing(out, seq, place), a_send.at[n, r], a_recv.at[n, r], (dp, to))

    def arrival(n, r):
        ref, out, place = sources[n]
        src = ring(seq, -r, 8)
        return remote(ref.at[:, pair_columns(pair)], landing(out, src, place), a_send.at[n, r],
                      a_recv.at[n, r], (dp, src))

    def pass_on(n, r, src):
        _, out, _ = sources[n]
        index = ring(seq, -r, 8)
        for side in range(2):
            go(remote(src, landing(out, index, SIDES[side][1]), h_send.at[side, n, r],
                      h_recv.at[side, n, r], beside[side]))

    def passed(n, r, side):
        out = sources[n][1]
        index = ring(flip(beside[side][0], pair), -r, 8)
        return remote(out.at[pl.ds(0, tokens), :], landing(out, index, SIDES[1 - side][1]),
                      h_send.at[1 - side, n, r], h_recv.at[1 - side, n, r], beside[side])

    far_first = (4, 3, 5, 2, 6, 1, 7)
    keeps = [keep]
    for n in range(3):
        ref, out, place = sources[n]
        mine = pltpu.make_async_copy(ref.at[:, pair_columns(pair)], landing(out, seq, place), own_sem.at[n])
        mine.start()
        keeps.append(mine)
    for n in range(2):
        for r in far_first:
            go(exchange(n, r))
    for n in range(2):
        pass_on(n, 0, sources[n][0].at[:, pair_columns(pair)])
    for r in far_first:
        go(exchange(2, r))

    for i in range(3):
        got_z(i).wait_recv()
        piece = part(0, i + 1, x)
        for j in range(1, 4):
            go(remote(piece, piece, wx_send.at[i, j - 1], wx_recv.at[i, j - 1], along_x(j)))
        send_across(i + 1, piece)
    for r in (1, 7):
        for n in range(2):
            arrival(n, r).wait_recv()
            pass_on(n, r, landing(sources[n][1], ring(seq, -r, 8), 1))
    for i in range(3):
        for j in range(1, 4):
            piece = part(0, i + 1, x_from(j))
            remote(piece, piece, wx_send.at[i, j - 1], wx_recv.at[i, j - 1], along_x(-j)).wait_recv()
        send_y(i + 1, whole(0, i + 1))
        send_sibling(0, i + 1, whole(0, i + 1))
    for r in (4, 3, 5, 2, 6):
        for n in range(2):
            arrival(n, r).wait_recv()
            pass_on(n, r, landing(sources[n][1], ring(seq, -r, 8), 1))
    for i in range(4):
        piece = part(3, i, x)
        remote(piece, piece, wq_send.at[i], wq_recv.at[i], along_y(2)).wait_recv()
        for j in range(1, 4):
            go(remote(piece, piece, wxx_send.at[i, j - 1], wxx_recv.at[i, j - 1], along_x(j)))
        for o in (1, 2):
            block = whole(o, i)
            remote(block, block, wy_send.at[o - 1, i], wy_recv.at[o - 1, i], along_y(y_off[o])).wait_recv()
            send_sibling(o, i, block)

    grads = []

    def project(o):
        for i in range(4):
            block = whole(o, i, False)
            remote(block, block, sib_send.at[o * 4 + i], sib_recv.at[o * 4 + i], sibling).wait_recv()
        base = 2 * lax.rem(y + y_off[o] + 4, 4)
        for b in range(2):
            g_stage[2 * o + b] = dotT(og_ref[...], w_out[rows_of(base + b, 256), :]).astype(BF16)
        for b in range(2):
            to = flip(dp, base + b)

            @pl.when(to != seq)
            def _():
                remote(g_stage.at[2 * o + b], g_out.at[rows_of(seq, tokens), :], g_send.at[2 * o + b],
                       g_recv.at[seq], (dp, to)).start()

            @pl.when(to == seq)
            def _():
                pltpu.make_async_copy(g_stage.at[2 * o + b], g_out.at[rows_of(seq, tokens), :], g_send.at[2 * o + b]).start()

            grads.append((2 * o + b, to))

    keep.wait()
    keeps.pop(0)
    og_load.wait()
    project(0)
    for i in range(4):
        for j in range(1, 4):
            piece = part(3, i, x_from(j))
            remote(piece, piece, wxx_send.at[i, j - 1], wxx_recv.at[i, j - 1], along_x(-j)).wait_recv()
        send_sibling(3, i, whole(3, i))
    project(1)
    project(2)
    project(3)

    for copy in keeps:
        copy.wait()
    for r in far_first:
        arrival(2, r).wait_recv()
    for n in range(2):
        for r in range(8):
            for side in range(2):
                passed(n, r, side).wait_recv()

    tiles = count_ref.shape[0]
    heads = q_buf.shape[1] // HD
    factor = HD ** -0.5
    base_tile = win_ref[0, 0] - tiles

    def place_of(t, j):
        return jnp.maximum(jnp.minimum(win_ref[t, j] - base_tile, 3 * tiles - 1), 0)

    for i in range(3 * tiles):
        for h in range(heads):
            k_tile[h, i] = k_out[i * TILE:(i + 1) * TILE, h * HD:(h + 1) * HD]
            v_tile[h, i] = v_out[i * TILE:(i + 1) * TILE, h * HD:(h + 1) * HD]

    def forward(h, t):
        cols = slice(h * HD, (h + 1) * HD)
        here = rows_of(t, TILE)
        q = q_buf[here, cols]
        top = None
        for j in range(WIN):
            scores = dotT(q, k_tile[h, place_of(t, j)])
            if j > 0:
                scores = scores + jnp.minimum(count_ref[t] - 1 - j, 0).astype(F32) * 1e30
            s_buf[j] = scores
            m = jnp.max(scores, axis=1, keepdims=True)
            top = m if top is None else jnp.maximum(top, m)
        total = jnp.zeros((TILE, 1), F32)
        acc = jnp.zeros((TILE, HD), F32)
        for j in range(WIN):
            e = jnp.exp2((s_buf[j] - top) * (factor * LOG2E))
            total = total + jnp.sum(e, axis=1, keepdims=True)
            eb = e.astype(BF16)
            e_buf[h * tiles + t, j] = eb
            acc = acc + dot(eb, v_tile[h, place_of(t, j)])
        inv = 1.0 / total
        attn = acc * inv
        attn_f[here, cols] = attn
        inv_f[here, cols] = jnp.broadcast_to(inv, (TILE, HD))
        attn_b[here, cols] = attn.astype(BF16)

    def backward(h, t):
        cols = slice(h * HD, (h + 1) * HD)
        here = rows_of(t, TILE)
        g = g_out[here, cols]
        gf = g.astype(F32)
        inv = inv_f[here, cols]
        centre = jnp.sum(gf * attn_f[here, cols], axis=1, keepdims=True)
        gs = (gf * inv).astype(BF16)
        qs = (q_buf[here, cols].astype(F32) * (inv * factor)).astype(BF16)
        dq = jnp.zeros((TILE, HD), F32)
        for j in range(WIN):
            at = place_of(t, j)
            dp_j = dotT(g, v_tile[h, at])
            eb = e_buf[h * tiles + t, j]
            ds = (eb.astype(F32) * (dp_j - centre)).astype(BF16)
            dq = dq + dot(ds, k_tile[h, at])
            pieces[0, t * WIN + j] = dot0(ds, qs)
            pieces[1, t * WIN + j] = dot0(eb, gs)
        dq_b[here, cols] = (dq * (inv * factor)).astype(BF16)

    def each_tile(what, h):
        def step(t, carry):
            what(h, t)
            return carry
        lax.fori_loop(0, tiles, step, 0)

    locals_ = []

    def local(src, dst, sem):
        copy = pltpu.make_async_copy(src, dst, sem)
        copy.start()
        locals_.append(copy)

    def head_columns(index, h):
        return pl.ds(pl.multiple_of(index * 256 + h * HD, HD), HD)

    def to_tokens(src, out, h, send, recv):
        cols = slice(h * HD, (h + 1) * HD)
        for r in far_first:
            to = ring(seq, r, 8)
            go(remote(src.at[rows_of(to, tokens), cols], out.at[:, head_columns(pair, h)], send.at[h, r], recv.at[h, r], (dp, to)))
        local(src.at[rows_of(seq, tokens), cols], out.at[:, head_columns(pair, h)], recv.at[h, 0])

    def from_heads(src, out, h, send, recv):
        for r in far_first:
            came = ring(seq, -r, 8)
            remote(src.at[rows_of(came, tokens), slice(h * HD, (h + 1) * HD)], out.at[:, head_columns(flip(dp, came), h)],
                   send.at[h, r], recv.at[h, r], (dp, came)).wait_recv()

    for h in range(heads):
        each_tile(forward, h)
        to_tokens(attn_b, tok, h, t_send, t_recv)

    for r in range(1, 8):
        src = ring(seq, -r, 8)
        remote(g_stage.at[0], g_out.at[rows_of(src, tokens), :], g_send.at[0], g_recv.at[src], (dp, src)).wait_recv()
    for slot, to in grads:

        @pl.when(to != seq)
        def _():
            remote(g_stage.at[slot], g_out.at[rows_of(seq, tokens), :], g_send.at[slot], g_recv.at[seq],
                   (dp, to)).wait_send()

        @pl.when(to == seq)
        def _():
            pltpu.make_async_copy(g_stage.at[slot], g_out.at[rows_of(seq, tokens), :], g_send.at[slot]).wait()

    empty = tiles * WIN
    for n in range(2):
        pieces[n, empty] = jnp.zeros((TILE, HD), F32)

    def found(t, tile):
        slot = empty
        for j in range(WIN):
            away = place_of(t, j) - tile
            slot = slot + (1 - jnp.minimum(away * away, 1)) * (t * WIN + j - empty)
        slot = jnp.maximum(slot, 0)
        return slot

    def fold(h):
        cols = slice(h * HD, (h + 1) * HD)

        def step(i, carry):
            here = rows_of(i, TILE)
            for place in range(3):
                slots = [found(t, place * tiles + i) for t in range(tiles)]
                for n in range(2):
                    total = pieces[n, slots[0]]
                    for slot in slots[1:]:
                        total = total + pieces[n, slot]
                    if place == 1:
                        own[n, here, cols] = total
                    else:
                        rim_buf[place // 2, n, here, cols] = total.astype(BF16)
            return carry

        lax.fori_loop(0, tiles, step, 0)

    into = (high, low)
    half = 4 * tokens

    def rim(h, n, side, part_of, device):
        at = rows_of(part_of, half)
        cols = slice(h * HD, (h + 1) * HD)
        return remote(rim_buf.at[side, n, at, cols], into[side].at[n, at, cols],
                      r_send.at[h, side * 2 + n, part_of], r_recv.at[h, side * 2 + n, part_of], device)

    for h in range(heads):
        each_tile(backward, h)
        to_tokens(dq_b, dq_out, h, d_send, d_recv)
        fold(h)
        for k in range(2):
            for side in range(2):
                first = 1 - beside[side][1] // 4
                for n in range(2):
                    go(rim(h, n, side, first if k == 0 else 1 - first, beside[side]))

    outs = (dk_out, dv_out)

    def finish(h):
        cols = slice(h * HD, (h + 1) * HD)
        for k in range(2):
            part_of = 1 - seq // 4 if k == 0 else seq // 4
            for side in range(2):
                for n in range(2):
                    rim(h, n, side, part_of, beside[1 - side]).wait_recv()
            at = rows_of(part_of, half)
            for n in range(2):
                stage[n, at, cols] = (own[n, at, cols] + low[n, at, cols].astype(F32) + high[n, at, cols].astype(F32)).astype(BF16)
            for r in (4, 3, 5, 2, 6, 1, 7):
                to = ring(seq, r, 8)

                @pl.when(to // 4 == part_of)
                def _():
                    for n in range(2):
                        summed(h, n, r, to).start()

        for n in range(2):
            local(stage.at[n, rows_of(seq, tokens), cols], outs[n].at[:, head_columns(pair, h)], s_recv.at[h, n, 0])

    def summed(h, n, r, to):
        return remote(stage.at[n, rows_of(to, tokens), slice(h * HD, (h + 1) * HD)], outs[n].at[:, head_columns(pair, h)],
                      s_send.at[h, n, r], s_recv.at[h, n, r], (dp, to))

    finish(0)
    for copy in locals_[:2]:
        copy.wait()
    for h in range(heads):
        from_heads(attn_b, tok, h, t_send, t_recv)
    cut = 512
    for c in range(o_out.shape[1] // cut):
        o_out[:, c * cut:(c + 1) * cut] = dot(tok[...], w_out[:, c * cut:(c + 1) * cut]).astype(BF16)
    finish(1)
    for copy in locals_[2:]:
        copy.wait()
    for h in range(heads):
        from_heads(dq_b, dq_out, h, d_send, d_recv)
        for r in far_first:
            came = ring(seq, -r, 8)
            for n in range(2):
                remote(stage.at[n, rows_of(came, tokens), slice(h * HD, (h + 1) * HD)],
                       outs[n].at[:, head_columns(flip(dp, came), h)], s_send.at[h, n, r], s_recv.at[h, n, r], (dp, came)).wait_recv()
                summed(h, n, r, ring(seq, r, 8)).wait_send()
    for copy in pending:
        copy.wait_send()


def body(query, key_in, value, out_weight, out_grad, windows, window_count):
    tokens, width = query.shape
    depth = out_weight.shape[1]
    tiles = windows.shape[0]
    rows = 8 * tokens
    vm = pl.BlockSpec(memory_space=pltpu.VMEM)
    sm = pl.BlockSpec(memory_space=pltpu.SMEM)
    hbm = pl.BlockSpec(memory_space=pl.ANY)
    sem = pltpu.SemaphoreType.DMA
    wide = jax.ShapeDtypeStruct((tokens, width), BF16)
    slab = (rows, 256)
    pairs = [(3, 8), (2, 2, 8), (8,), (3,), (3, 3), (2, 4), (4,), (4, 3), (16,), (2, 8), (2, 8), (2, 4, 2), (2, 2, 8)]
    scratch = [
        (slab, BF16), ((3 * rows, 256), BF16), ((3 * rows, 256), BF16), (slab, BF16), ((width, depth), BF16),
        ((tokens, depth), BF16), ((8, tokens, 256), BF16), ((WIN, TILE, TILE), F32), ((2 * tiles, WIN, TILE, TILE), BF16),
        (slab, F32), (slab, F32), (slab, BF16), (slab, BF16), ((2, tiles * WIN + 1, TILE, HD), F32), ((2,) + slab, F32),
        ((2, 3 * tiles, TILE, HD), BF16), ((2, 3 * tiles, TILE, HD), BF16), ((2, 2) + slab, BF16), ((2,) + slab, BF16), ((2,) + slab, BF16), ((2,) + slab, BF16), ((tokens, width), BF16),
    ]
    return tuple(pl.pallas_call(
        layer,
        out_shape=[jax.ShapeDtypeStruct((tokens, depth), BF16), wide, wide, wide],
        in_specs=[sm, sm] + [hbm] * 5,
        out_specs=[vm] * 4,
        scratch_shapes=[pltpu.VMEM(*p) for p in scratch]
        + [sem(p) for p in pairs for _ in range(2)] + [sem((5,))],
        compiler_params=pltpu.CompilerParams(collective_id=0, has_side_effects=True, vmem_limit_bytes=63 << 20),
    )(windows, window_count, query, key_in, value, out_weight, out_grad))


def solution(mesh):
    both = P(("dp", "seq"), None)
    return jax.shard_map(
        body, mesh=mesh, check_vma=False,
        in_specs=(both, both, both, P("dp", None), both, P("dp", None), P("dp")),
        out_specs=(both, both, both, both),
    )
```
